32 devices in a mesh: groups: 2 (over x), inst: 4 (over z), tp: 4 (over y, core).
Axes of the slice: x: 2, y: 2, z: 4, core: 2. Of those that a mesh axis runs over, the one named last changes fastest.
Arguments:
- qkv_first: bfloat16 [48, 10240], P(('groups', 'inst'), 'tp'), parts along dimension 0, may hold values from -5 to 5
- qkv_second: bfloat16 [48, 10240], P(('groups', 'inst'), 'tp'), parts along dimension 0, may hold values from -5 to 5
- w_out: bfloat16 [8192, 8192], P(None, 'tp'), may hold values from -0.5 to 0.5
- kv_cache: bfloat16 [512, 2, 16, 1024], P(('groups', 'inst', 'tp')), parts along dimension 0, may hold values from -4096 to 4096
- lengths: int32 [48], P('groups'), parts along dimension 0, may hold values from 4 to 126, as said below
- page_table: int32 [48, 8], P(('groups', 'inst')), parts along dimension 0, may hold values from -1 to 63, as said below
- moves: int32 [8, 2], P('groups'), parts along dimension 0, may hold values from 0 to 23, as said below
- dest_pages: int32 [8, 8], P('groups'), parts along dimension 0, may hold values from 0 to 63, as said below
Outputs:
- out_first: bfloat16 [48, 8192], P(('groups', 'inst'), 'tp'), parts along dimension 0
- out_second: bfloat16 [48, 8192], P(('groups', 'inst'), 'tp'), parts along dimension 0
- kv_out: bfloat16 [512, 2, 16, 1024], P(('groups', 'inst', 'tp')), parts along dimension 0
The draws below stay inside these ranges and needn't reach their ends.
There are 2 independent parts, one for each index of `groups`. The reference program is written for one: setup_inputs(seed, part) draws one part's arguments, and reference() takes and returns one part's arrays. A program takes and returns all parts, laid end to end along the dimension named above; an argument that names none is the same for every part. Nothing has to cross between parts.
Inputs may be any that keep to these rules, and one draw needn't show every extreme that they name: Half of the instances, drawn afresh, are heavy: lengths of their requests run from 64 to 126, those of the other instances from 4 to 16. Entry j of request r is a page of its instance's pool for j < ceil((lengths[r] + 2) / 16) and -1 after; such a page p has floor(p / 16) = j mod (4); no pool page is named twice by page_table and dest_pages together. Row i moves request moves[i, 0], a number from 0 to 23, to instance moves[i, 1], a number from 0 to 3; every heavy instance sends exactly one request to every other instance, those are the light ones, and a moved request's length is at least (7) * 16 - 1. `dest_pages`: entry j of row i, for every j < 8, is a page p of the destination's pool that page_table leaves free, with floor(p / 16) = j mod (4).
All inputs are finite; a program needn't handle non-finite values.
Results may differ from the reference program's by a relative error of at most 0.015.
Values may be sent and summed in bfloat16 or wider, within the bound.
A program may use at most 64 MiB of HBM per device.

```python
import math
from functools import partial
import jax
import jax.numpy as jnp
from jax import lax

D = 8192
QUERY_HEADS = 64
KEY_VALUE_HEADS = 8
HEAD_SIZE = 128
PAGE_POSITIONS = 16
MP = 2
R_INST = 6
QKV = 10240
REQUEST_PAGES = 8
POOL_DEV = 16
POOL_INST = 64
STORE_PAGES = 256
R = 24
MOVED_REQUESTS = 4


def permuted(sub_key, count):
    return jax.random.permutation(sub_key, count)


def layout(key):
    base_key = jax.random.fold_in(key, 7001)
    key_order, key_slots, key_heavy, key_light, key_long, key_pool, key_shuffle = jax.random.split(base_key, 7)
    inst_count = R // R_INST
    rank_count = REQUEST_PAGES // MP
    half_count = inst_count // 2
    page_extent = REQUEST_PAGES * PAGE_POSITIONS
    inst_order = jax.random.permutation(key_order, inst_count).astype(jnp.int32)
    heavy_flag = jnp.zeros((inst_count,), jnp.int32).at[inst_order[:half_count]].set(1)
    slot_order = jax.vmap(partial(permuted, count=R_INST))(jax.random.split(key_slots, inst_count)).astype(jnp.int32)
    slot_place = jnp.argsort(slot_order, axis=1).astype(jnp.int32)
    heavy_len = jax.random.randint(key_heavy, (inst_count, R_INST), page_extent // 2, page_extent - 1)
    light_len = jax.random.randint(key_light, (inst_count, R_INST), 4, page_extent // 8 + 1)
    long_len = jax.random.randint(key_long, (inst_count, R_INST), (REQUEST_PAGES - 1) * PAGE_POSITIONS - 1, page_extent - 1)
    is_heavy = heavy_flag[:, None] == 1
    moved_flag = is_heavy & (slot_place < half_count)
    lengths = jnp.where(moved_flag, long_len, jnp.where(is_heavy, heavy_len, light_len)).astype(jnp.int32)
    pool_order = jax.vmap(partial(permuted, count=POOL_DEV))(jax.random.split(key_pool, inst_count * rank_count))
    pool_order = pool_order.reshape(inst_count, rank_count, POOL_DEV).astype(jnp.int32)
    page_ids = jnp.arange(REQUEST_PAGES, dtype=jnp.int32)
    page_rank = page_ids % rank_count
    page_depth = page_ids // rank_count
    slot_ids = jnp.arange(R_INST, dtype=jnp.int32)
    inst_ids = jnp.arange(inst_count, dtype=jnp.int32)
    local_index = slot_ids[:, None] * MP + page_depth[None, :]
    local_page = pool_order[inst_ids[:, None, None], page_rank[None, None, :], local_index[None, :, :]]
    needed = (lengths + 2 + PAGE_POSITIONS - 1) // PAGE_POSITIONS
    table = jnp.where(page_ids[None, None, :] < needed[:, :, None], page_rank[None, None, :] * POOL_DEV + local_page, -1)
    table = table.reshape(R, REQUEST_PAGES).astype(jnp.int32)
    heavy_pos = jnp.arange(half_count, dtype=jnp.int32)[:, None]
    light_pos = jnp.arange(half_count, dtype=jnp.int32)[None, :]
    heavy_inst = inst_order[heavy_pos[:, 0]][:, None]
    light_inst = inst_order[half_count + light_pos[0]][None, :]
    moved_slot = slot_order[heavy_inst, light_pos]
    request_ids = jnp.broadcast_to(heavy_inst * R_INST + moved_slot, (half_count, half_count))
    dest_inst = jnp.broadcast_to(light_inst, (half_count, half_count))
    incoming = (R_INST + heavy_pos[:, :, None]) * MP + page_depth[None, None, :]
    incoming = jnp.broadcast_to(incoming, (half_count, half_count, REQUEST_PAGES))
    dest_local = pool_order[dest_inst[:, :, None], page_rank[None, None, :], incoming]
    dest_table = page_rank[None, None, :] * POOL_DEV + dest_local
    shuffle = jax.random.permutation(key_shuffle, MOVED_REQUESTS)
    moves = jnp.stack([request_ids.reshape(-1), dest_inst.reshape(-1)], axis=1)[shuffle].astype(jnp.int32)
    dest_table = dest_table.reshape(MOVED_REQUESTS, REQUEST_PAGES)[shuffle].astype(jnp.int32)
    return (lengths.reshape(R), table, moves, dest_table)


def token_drawn(key, which):
    step_key = jax.random.fold_in(key, 9100 + which)
    key_body = jax.random.fold_in(step_key, 1)
    return jnp.clip(jax.random.normal(key_body, (R, QKV), jnp.float32), -5.0, 5.0)


def draw_qkv_first(key, part):
    return token_drawn(key, 1).astype(jnp.bfloat16)


def draw_qkv_second(key, part):
    return token_drawn(key, 2).astype(jnp.bfloat16)


def draw_kv_cache(key, part):
    store_key = jax.random.fold_in(key, 9300)
    memory_shape = (STORE_PAGES, 2, PAGE_POSITIONS, KEY_VALUE_HEADS * HEAD_SIZE)
    return jnp.clip(jax.random.normal(store_key, memory_shape, jnp.float32), -5.0, 5.0).astype(jnp.bfloat16)


def draw_lengths(key, part):
    return layout(key)[0]


def draw_page_table(key, part):
    return layout(key)[1]


def draw_moves(key, part):
    return layout(key)[2]


def draw_dest_pages(key, part):
    return layout(key)[3]


def levels(rng, dims, cuts, least, top_value):
    def one(position, parts):
        steps = jax.random.uniform(jax.random.fold_in(jax.random.fold_in(rng, 6), position), (parts,), jnp.float32, least / len(cuts), top_value / len(cuts))
        return jnp.repeat(jnp.exp(steps), dims[position] // parts).reshape((-1,) + (1,) * (len(dims) - position - 1))

    factor_of = one(*cuts[0])
    for cut in cuts[1:]:
        factor_of = factor_of * one(*cut)
    return factor_of


def bell_draw(key, dims, width, bound, shards=(), kind=jnp.bfloat16):
    entries = jax.random.normal(key, dims, jnp.float32) * width
    if len(shards) > 0:
        entries = levels(key, dims, shards, -0.22, 0.18) * entries
    return jnp.clip(entries, min=-bound, max=bound).astype(kind)


def setup_inputs(seed: int = 0, part: int = 0) -> dict:
    seeds = jax.random.split(jax.random.key(seed), 9)
    part_keys = jax.random.split(jax.random.fold_in(seeds[8], part), 9)
    return {
        "qkv_first": draw_qkv_first(jax.random.fold_in(jax.random.fold_in(seeds[8], part), 71), part),
        "qkv_second": draw_qkv_second(jax.random.fold_in(jax.random.fold_in(seeds[8], part), 71), part),
        "w_out": bell_draw(seeds[2], (QUERY_HEADS * HEAD_SIZE, D), HEAD_SIZE ** -0.5, 0.5, ((1, 4),)),
        "kv_cache": draw_kv_cache(jax.random.fold_in(jax.random.fold_in(seeds[8], part), 71), part),
        "lengths": draw_lengths(jax.random.fold_in(jax.random.fold_in(seeds[8], part), 71), part),
        "page_table": draw_page_table(jax.random.fold_in(jax.random.fold_in(seeds[8], part), 71), part),
        "moves": draw_moves(jax.random.fold_in(jax.random.fold_in(seeds[8], part), 71), part),
        "dest_pages": draw_dest_pages(jax.random.fold_in(jax.random.fold_in(seeds[8], part), 71), part),
    }


def attend(single_query, page_tile, live_count):
    group_width = QUERY_HEADS // KEY_VALUE_HEADS
    gathered_keys = page_tile[:, 0].reshape(REQUEST_PAGES * PAGE_POSITIONS, KEY_VALUE_HEADS, HEAD_SIZE).astype(jnp.float32)
    gathered_values = page_tile[:, 1].reshape(REQUEST_PAGES * PAGE_POSITIONS, KEY_VALUE_HEADS, HEAD_SIZE).astype(jnp.float32)
    heads_of_query = single_query.astype(jnp.float32).reshape(KEY_VALUE_HEADS, group_width, HEAD_SIZE)
    logit_scores = jnp.einsum('kgd,tkd->kgt', heads_of_query, gathered_keys, precision=lax.Precision.HIGHEST) / math.sqrt(HEAD_SIZE)
    visible = jnp.arange(REQUEST_PAGES * PAGE_POSITIONS, dtype=jnp.int32) < live_count
    logit_scores = jnp.where(visible[None, None, :], logit_scores, -jnp.inf)
    row_top = lax.optimization_barrier(jnp.max(logit_scores, axis=2, keepdims=True))
    exponent = jnp.where(visible[None, None, :], jnp.exp(logit_scores - row_top), 0.0)
    row_total = lax.optimization_barrier(jnp.sum(exponent, axis=2))
    weights = lax.optimization_barrier(exponent.astype(jnp.bfloat16)).astype(jnp.float32)
    summed = jnp.einsum('kgt,tkd->kgd', weights, gathered_values, precision=lax.Precision.HIGHEST)
    return (summed / row_total[:, :, None]).reshape(QUERY_HEADS * HEAD_SIZE).astype(jnp.bfloat16)

def write_tokens(paged_memory, token_rows, store_rows, positions):
    kv_start = QUERY_HEADS * HEAD_SIZE
    key_value_width = KEY_VALUE_HEADS * HEAD_SIZE
    new_keys = token_rows[:, kv_start:kv_start + key_value_width]
    new_values = token_rows[:, kv_start + key_value_width:kv_start + 2 * key_value_width]
    page_index = (positions // PAGE_POSITIONS).astype(jnp.int32)
    target_rows = jnp.take_along_axis(store_rows, page_index[:, None], axis=1)[:, 0]
    offsets = (positions % PAGE_POSITIONS).astype(jnp.int32)
    paged_memory = paged_memory.at[target_rows, 0, offsets].set(new_keys)
    paged_memory = paged_memory.at[target_rows, 1, offsets].set(new_values)
    return paged_memory

def decode_layer(paged_memory, token_rows, store_rows, counts, w_out):

    def attend_one(request):
        single_query, index_row, live_count = request
        page_tile = paged_memory[jnp.maximum(index_row, 0)]
        return attend(single_query, page_tile, live_count)
    mixed = lax.map(attend_one, (token_rows[:, :QUERY_HEADS * HEAD_SIZE], store_rows, counts))
    return jnp.dot(mixed, w_out, preferred_element_type=jnp.float32).astype(jnp.bfloat16)

def reference(qkv_first, qkv_second, w_out, kv_cache, lengths, page_table, moves, dest_pages):
    home_rows = jnp.arange(R, dtype=jnp.int32) // R_INST * POOL_INST
    store_rows = jnp.where(page_table >= 0, page_table + home_rows[:, None], -1).astype(jnp.int32)
    paged_memory = write_tokens(kv_cache, qkv_first, store_rows, lengths)
    out_first = decode_layer(paged_memory, qkv_first, store_rows, lengths + 1, w_out)
    movers = moves[:, 0]
    source_instances = store_rows[movers]
    targets = (moves[:, 1][:, None] * POOL_INST + dest_pages).astype(jnp.int32)
    paged_memory = paged_memory.at[targets.reshape(-1)].set(paged_memory[source_instances.reshape(-1)])
    paged_memory = paged_memory.at[source_instances.reshape(-1)].set(jnp.zeros((MOVED_REQUESTS * REQUEST_PAGES, 2, PAGE_POSITIONS, KEY_VALUE_HEADS * HEAD_SIZE), jnp.bfloat16))
    store_rows = store_rows.at[movers].set(targets)
    paged_memory = write_tokens(paged_memory, qkv_second, store_rows, lengths + 1)
    out_second = decode_layer(paged_memory, qkv_second, store_rows, lengths + 2, w_out)
    return (out_first, out_second, paged_memory)
```

```python
import functools
import math

import jax
import jax.numpy as jnp
from jax import lax
from jax.experimental import pallas as pl
from jax.experimental.pallas import tpu as pltpu
from jax.sharding import PartitionSpec as P

QUERY_HEADS = 64
KEY_VALUE_HEADS = 8
HEAD_SIZE = 128
NEG_LARGE = -1e30
FAR = 1 << 30
MESH = pl.DeviceIdType.MESH


def kernel(
    sizes,
    x_ref,
    aux_ref,
    moves,
    table,
    dests,
    cache_hbm,
    w_hbm,
    o1_ref,
    o2_ref,
    kv_hbm,
    full,
    cache,
    part,
    stat,
    land,
    land_stat,
    mixed,
    acc,
    wbuf,
    outgoing,
    arrived,
    cache_sem,
    w_sem,
    send_sem,
    recv_sem,
    page_send,
    page_recv,
):
    tp, inst, row_count, max_pages, move_count = sizes
    rank = lax.axis_index("tp")
    me = lax.axis_index("inst")
    rows, cw = x_ref.shape
    pages, _, extent, width = cache.shape
    spots = pages * extent
    heads_per = QUERY_HEADS // tp
    group = QUERY_HEADS // KEY_VALUE_HEADS
    hd = HEAD_SIZE
    per_rank = max_pages // tp
    chunk = wbuf.shape[1]

    load_cache = pltpu.make_async_copy(cache_hbm, cache, cache_sem.at[0])
    load_cache.start()
    for t in range(tp):
        pltpu.make_async_copy(
            w_hbm.at[pl.ds(t * chunk, chunk), :], wbuf.at[t], w_sem.at[t]
        ).start()

    barrier = pltpu.get_barrier_semaphore()
    for k in range(1, tp):
        pl.semaphore_signal(
            barrier, inc=1, device_id={"tp": lax.rem(rank + k, tp)}, device_id_type=MESH
        )
    for k in range(1, inst):
        pl.semaphore_signal(
            barrier, inc=1, device_id={"inst": lax.rem(me + k, inst)}, device_id_type=MESH
        )
    pl.semaphore_wait(barrier, tp - 1 + inst - 1)

    def exchange(phase, k, src, dst):
        return pltpu.make_async_remote_copy(
            src_ref=src,
            dst_ref=dst,
            send_sem=send_sem.at[phase, k],
            recv_sem=recv_sem.at[phase, k],
            device_id={"tp": lax.rem(rank + k, tp)},
            device_id_type=MESH,
        )

    started = []
    gathers = [exchange(0, k, x_ref, full.at[rank]) for k in range(1, tp)]
    for copy in gathers:
        copy.start()
    started += gathers
    full[rank] = x_ref[...]

    column = lax.broadcasted_iota(jnp.int32, (rows, spots), 1)
    page_id = column // extent + rank * pages
    offset = lax.rem(column, extent)
    pos = jnp.full((rows, spots), FAR, jnp.int32)
    for n in range(max_pages):
        pos = jnp.where(aux_ref[:, n : n + 1] == page_id, n * extent + offset, pos)
    target = aux_ref[:, max_pages : max_pages + 1]
    visible = pos <= target
    hit = jnp.where(pos == target, 1.0, 0.0)
    hit_t = hit.T.astype(jnp.bfloat16)
    written = jnp.dot(
        hit_t, jnp.ones((rows, hd), jnp.bfloat16), preferred_element_type=jnp.float32
    ) > 0.5
    visible_all = jnp.concatenate([visible.astype(jnp.int32)] * group, axis=0) > 0

    sources = [moves[m, 0] // row_count for m in range(move_count)]
    send_has, send_page, recv_has, recv_page = [], [], [], []
    for k in range(1, inst):
        dst = lax.rem(me + k, inst)
        src = lax.rem(me + inst - k, inst)
        out_has = jnp.int32(0)
        out_row = jnp.int32(0)
        in_has = jnp.int32(0)
        in_move = jnp.int32(0)
        for m in range(move_count):
            goes = (sources[m] == me) & (moves[m, 1] == dst)
            comes = (sources[m] == src) & (moves[m, 1] == me)
            out_has = jnp.where(goes, 1, out_has)
            out_row = jnp.where(goes, moves[m, 0] - me * row_count, out_row)
            in_has = jnp.where(comes, 1, in_has)
            in_move = jnp.where(comes, m, in_move)
        for j in range(per_rank):
            send_has.append(out_has)
            found = table[out_row, rank + tp * j] - rank * pages
            send_page.append(jnp.clip(found, 0, pages - 1))
            recv_has.append(in_has)
            recv_page.append(dests[in_move, rank + tp * j] - rank * pages)

    load_cache.wait()
    for copy in gathers:
        copy.wait_recv()

    def token_columns(c):
        return full[c // cw, :, c % cw : c % cw + hd]

    base = QUERY_HEADS * hd
    for which in range(2):
        for g in range(KEY_VALUE_HEADS):
            fresh = token_columns(base + which * width + g * hd)
            placed = jnp.dot(hit_t, fresh, preferred_element_type=jnp.float32)
            old = cache[:, which, :, g * hd : (g + 1) * hd].reshape(spots, hd)
            new = jnp.where(written, placed, old.astype(jnp.float32)).astype(jnp.bfloat16)
            cache[:, which, :, g * hd : (g + 1) * hd] = new.reshape(pages, extent, hd)

    page_copies = []
    for k in range(1, inst):
        for j in range(per_rank):
            outgoing[k - 1, j] = cache[send_page[(k - 1) * per_rank + j]]
        copy = pltpu.make_async_remote_copy(
            src_ref=outgoing.at[k - 1],
            dst_ref=arrived.at[k - 1],
            send_sem=page_send.at[k - 1],
            recv_sem=page_recv.at[k - 1],
            device_id={"inst": lax.rem(me + k, inst)},
            device_id_type=MESH,
        )
        copy.start()
        page_copies.append(copy)

    scale = 1.0 / math.sqrt(hd)
    lane = lax.broadcasted_iota(jnp.int32, (rows, 128), 1)
    stats = [jnp.zeros((rows, 128), jnp.float32) for _ in range(tp)]
    for g in range(KEY_VALUE_HEADS):
        queries = jnp.concatenate(
            [token_columns((g * group + j) * hd) for j in range(group)], axis=0
        )
        keys = cache[:, 0, :, g * hd : (g + 1) * hd].reshape(spots, hd)
        values = cache[:, 1, :, g * hd : (g + 1) * hd].reshape(spots, hd)
        scores = (
            lax.dot_general(
                queries, keys, (((1,), (1,)), ((), ())), preferred_element_type=jnp.float32
            )
            * scale
        )
        scores = jnp.where(visible_all, scores, NEG_LARGE)
        top = jnp.max(scores, axis=1, keepdims=True)
        exponent = jnp.where(visible_all, jnp.exp(scores - top), 0.0)
        total = jnp.sum(exponent, axis=1, keepdims=True)
        summed = jnp.dot(
            exponent.astype(jnp.bfloat16), values, preferred_element_type=jnp.float32
        ).astype(jnp.bfloat16)
        for j in range(group):
            h = g * group + j
            t, at = h // heads_per, h % heads_per
            take = slice(j * rows, (j + 1) * rows)
            part[t, :, at * hd : (at + 1) * hd] = summed[take]
            stats[t] = jnp.where(
                lane == at, top[take], jnp.where(lane == 64 + at, total[take], stats[t])
            )
    for t in range(tp):
        stat[t] = stats[t]

    sums = []
    for k in range(1, tp):
        peer = lax.rem(rank + k, tp)
        sums.append(
            (
                exchange(1, k, part.at[peer], land.at[k - 1]),
                exchange(2, k, stat.at[peer], land_stat.at[k - 1]),
            )
        )
    for pair in sums:
        pair[1].start()
        pair[0].start()
        started += pair
    for pair in sums:
        pair[1].wait_recv()
        pair[0].wait_recv()

    all_stats = [stat[rank]] + [land_stat[k] for k in range(tp - 1)]
    highest = functools.reduce(jnp.maximum, all_stats)
    scales = [jnp.exp(s - highest) for s in all_stats]
    whole = functools.reduce(
        jnp.add, [pltpu.roll(s, 64, 1) * f for s, f in zip(all_stats, scales)]
    )
    whole = jnp.where(whole > 0.0, whole, 1.0)
    factors = [f / whole for f in scales]
    for at in range(heads_per):
        span = slice(at * hd, (at + 1) * hd)
        merged = part[rank, :, span].astype(jnp.float32) * factors[0][:, at : at + 1]
        for k in range(tp - 1):
            merged += land[k, :, span].astype(jnp.float32) * factors[k + 1][:, at : at + 1]
        mixed[rank, :, span] = merged.astype(jnp.bfloat16)

    shares = [exchange(3, k, mixed.at[rank], mixed.at[rank]) for k in range(1, tp)]
    for copy in shares:
        copy.start()
    started += shares

    columns = wbuf.shape[2]
    tile = min(256, columns)

    def project(k):
        t = lax.rem(rank + tp - k, tp)
        pltpu.make_async_copy(
            w_hbm.at[pl.ds(0, chunk), :], wbuf.at[t], w_sem.at[t]
        ).wait()

        def step(n, carry):
            span = pl.ds(pl.multiple_of(n * tile, tile), tile)
            product = jnp.dot(
                mixed[t], wbuf[t, :, span], preferred_element_type=jnp.float32
            )
            if k == 0:
                acc[:, span] = product
            else:
                acc[:, span] += product
            return carry

        lax.fori_loop(0, columns // tile, step, 0)

    project(0)
    for k in range(1, tp):
        shares[k - 1].wait_recv()
        project(k)

    for copy in page_copies:
        copy.wait_recv()
    slots = (inst - 1) * per_rank
    for p in range(pages):
        source = jnp.int32(0)
        lands = jnp.int32(0)
        freed = jnp.int32(0)
        for i in range(slots):
            match = (recv_has[i] == 1) & (recv_page[i] == p)
            source = jnp.where(match, i, source)
            lands = jnp.where(match, 1, lands)
            freed = jnp.where((send_has[i] == 1) & (send_page[i] == p), 1, freed)
        kept = jnp.where(freed == 1, jnp.zeros((), jnp.bfloat16), cache[p])
        if slots:
            kept = jnp.where(
                lands == 1, arrived[source // per_rank, lax.rem(source, per_rank)], kept
            )
        cache[p] = kept
    store = pltpu.make_async_copy(cache, kv_hbm, cache_sem.at[1])
    store.start()
    o1_ref[...] = acc[0:row_count].astype(jnp.bfloat16)
    o2_ref[...] = acc[row_count : 2 * row_count].astype(jnp.bfloat16)
    for copy in started + page_copies:
        copy.wait_send()
    store.wait()


def local(qkv_first, qkv_second, w_out, kv_cache, lengths, page_table, moves, dest_pages):
    tp = lax.axis_size("tp")
    inst = lax.axis_size("inst")
    me = lax.axis_index("inst")
    row_count, max_pages = page_table.shape
    rows = -(-2 * row_count // 16) * 16
    spare = rows - 2 * row_count
    cw = qkv_first.shape[1]
    columns = w_out.shape[1]
    depth = QUERY_HEADS * HEAD_SIZE
    share = depth // tp
    per_rank = max_pages // tp
    mine = lax.dynamic_slice_in_dim(lengths, me * row_count, row_count)
    tokens = jnp.concatenate(
        [qkv_first, qkv_second, jnp.zeros((spare, cw), qkv_first.dtype)], axis=0
    )
    targets = jnp.concatenate([mine, mine + 1, jnp.full((spare,), -5, jnp.int32)])
    owners = jnp.concatenate(
        [page_table, page_table, jnp.full((spare, max_pages), -1, jnp.int32)], axis=0
    )
    aux = jnp.concatenate([owners, targets[:, None]], axis=1)
    sizes = (tp, inst, row_count, max_pages, moves.shape[0])
    vmem = pl.BlockSpec(memory_space=pltpu.VMEM)
    smem = pl.BlockSpec(memory_space=pltpu.SMEM)
    anywhere = pl.BlockSpec(memory_space=pl.ANY)
    page = kv_cache.shape[1:]
    bf16, f32 = jnp.bfloat16, jnp.float32
    others = max(tp - 1, 1)
    far = max(inst - 1, 1)
    dma = pltpu.SemaphoreType.DMA
    return pl.pallas_call(
        functools.partial(kernel, sizes),
        out_shape=(
            jax.ShapeDtypeStruct((row_count, columns), bf16),
            jax.ShapeDtypeStruct((row_count, columns), bf16),
            jax.ShapeDtypeStruct(kv_cache.shape, bf16),
        ),
        in_specs=[vmem, vmem, smem, smem, smem, anywhere, anywhere],
        out_specs=(vmem, vmem, anywhere),
        scratch_shapes=[
            pltpu.VMEM((tp, rows, cw), bf16),
            pltpu.VMEM(kv_cache.shape, bf16),
            pltpu.VMEM((tp, rows, share), bf16),
            pltpu.VMEM((tp, rows, 128), f32),
            pltpu.VMEM((others, rows, share), bf16),
            pltpu.VMEM((others, rows, 128), f32),
            pltpu.VMEM((tp, rows, share), bf16),
            pltpu.VMEM((rows, columns), f32),
            pltpu.VMEM((tp, share, columns), bf16),
            pltpu.VMEM((far, per_rank) + page, bf16),
            pltpu.VMEM((far, per_rank) + page, bf16),
            dma((2,)),
            dma((tp,)),
            dma((4, tp)),
            dma((4, tp)),
            dma((far,)),
            dma((far,)),
        ],
        compiler_params=pltpu.CompilerParams(
            collective_id=0, has_side_effects=True, vmem_limit_bytes=56 << 20
        ),
    )(tokens, aux, moves, page_table, dest_pages, kv_cache, w_out)


def solution(mesh):
    placed = (
        P(("groups", "inst"), "tp"),
        P(("groups", "inst"), "tp"),
        P(None, "tp"),
        P(("groups", "inst", "tp"), None, None, None),
        P("groups"),
        P(("groups", "inst"), None),
        P("groups", None),
        P("groups", None),
    )
    return jax.shard_map(
        local,
        mesh=mesh,
        in_specs=placed,
        out_specs=(
            P(("groups", "inst"), "tp"),
            P(("groups", "inst"), "tp"),
            P(("groups", "inst", "tp"), None, None, None),
        ),
        check_vma=False,
    )
```

```python
import functools
import math

import jax
import jax.numpy as jnp
from jax import lax
from jax.experimental import pallas as pl
from jax.experimental.pallas import tpu as pltpu
from jax.sharding import PartitionSpec as P

QUERY_HEADS = 64
KEY_VALUE_HEADS = 8
HEAD_SIZE = 128
NEG_LARGE = -1e30
FAR = 1 << 30
MESH = pl.DeviceIdType.MESH


def partner(rank, k, count):
    if count & (count - 1):
        return lax.rem(rank + k, count), lax.rem(rank + count - k, count)
    other = jnp.int32(0)
    bit = 1
    while bit < count:
        mine = (rank // bit) % 2
        other = other + bit * ((1 - mine) if (k // bit) % 2 else mine)
        bit *= 2
    return other, other


def kernel(
    sizes,
    first_hbm,
    second_hbm,
    lengths_hbm,
    moves_hbm,
    table_hbm,
    dests_hbm,
    cache_hbm,
    w_hbm,
    o1_ref,
    o2_ref,
    cache,
    first,
    second,
    table_v,
    lengths,
    moves,
    table,
    dests,
    x_ref,
    full,
    part,
    stat,
    land,
    land_stat,
    mixed,
    acc,
    wbuf,
    outgoing,
    arrived,
    small_sem,
    w_sem,
    send_sem,
    recv_sem,
    page_send,
    page_recv,
):
    tp, inst, row_count, max_pages, move_count = sizes
    rank = lax.axis_index("tp")
    me = lax.axis_index("inst")
    rows, cw = x_ref.shape
    pages, _, extent, width = cache.shape
    spots = pages * extent
    heads_per = QUERY_HEADS // tp
    group = QUERY_HEADS // KEY_VALUE_HEADS
    hd = HEAD_SIZE
    per_rank = max_pages // tp
    chunk = wbuf.shape[1]
    peers = [partner(rank, k, tp)[0] for k in range(tp)]
    froms = [partner(rank, k, tp)[1] for k in range(tp)]

    loads = [
        pltpu.make_async_copy(src, dst, small_sem.at[i])
        for i, (src, dst) in enumerate(
            [
                (first_hbm, first),
                (second_hbm, second),
                (table_hbm, table_v),
                (lengths_hbm, lengths),
                (moves_hbm, moves),
                (table_hbm, table),
                (dests_hbm, dests),
                (cache_hbm, cache),
            ]
        )
    ]
    for load in loads:
        load.start()
    barrier = pltpu.get_barrier_semaphore()
    for k in range(1, tp):
        pl.semaphore_signal(
            barrier, inc=1, device_id={"tp": lax.rem(rank + k, tp)}, device_id_type=MESH
        )
    for k in range(1, inst):
        pl.semaphore_signal(
            barrier, inc=1, device_id={"inst": lax.rem(me + k, inst)}, device_id_type=MESH
        )
    for t in range(tp):
        pltpu.make_async_copy(
            w_hbm.at[pl.ds(t * chunk, chunk), :], wbuf.at[t], w_sem.at[t]
        ).start()
    loads[0].wait()
    loads[1].wait()
    pieces = [first[...].astype(jnp.float32), second[...].astype(jnp.float32)]
    if rows > 2 * row_count:
        pieces.append(jnp.zeros((rows - 2 * row_count, cw), jnp.float32))
    tokens = jnp.concatenate(pieces, axis=0).astype(jnp.bfloat16)
    x_ref[...] = tokens
    full[rank] = tokens
    pl.semaphore_wait(barrier, tp - 1 + inst - 1)

    def exchange(phase, k, src, dst):
        return pltpu.make_async_remote_copy(
            src_ref=src,
            dst_ref=dst,
            send_sem=send_sem.at[phase, k],
            recv_sem=recv_sem.at[phase, k],
            device_id={"tp": peers[k]},
            device_id_type=MESH,
        )

    started = []
    gathers = [exchange(0, k, x_ref, full.at[rank]) for k in reversed(range(1, tp))]
    for copy in gathers:
        copy.start()
    started += gathers
    for load in loads[2:7]:
        load.wait()

    column = lax.broadcasted_iota(jnp.int32, (row_count, spots), 1)
    page_id = column // extent + rank * pages
    offset = lax.rem(column, extent)
    pos = jnp.full((row_count, spots), FAR, jnp.int32)
    for n in range(max_pages):
        pos = jnp.where(table_v[:, n : n + 1] == page_id, n * extent + offset, pos)
    spread = [pos, pos]
    if rows > 2 * row_count:
        spread.append(jnp.full((rows - 2 * row_count, spots), FAR, jnp.int32))
    pos = jnp.concatenate(spread, axis=0)
    row_id = lax.broadcasted_iota(jnp.int32, (rows, spots), 0)
    target = jnp.full((rows, spots), -5, jnp.int32)
    for r in range(row_count):
        length = lengths[me * row_count + r]
        target = jnp.where(row_id == r, length, target)
        target = jnp.where(row_id == row_count + r, length + 1, target)
    visible = pos <= target
    hit = jnp.where(pos == target, 1.0, 0.0)
    hit_t = hit.T.astype(jnp.bfloat16)
    written = jnp.dot(
        hit_t, jnp.ones((rows, hd), jnp.bfloat16), preferred_element_type=jnp.float32
    ) > 0.5
    visible_all = jnp.concatenate([visible.astype(jnp.int32)] * group, axis=0) > 0

    sources = [moves[0, m] // row_count for m in range(move_count)]
    send_has, send_page, recv_has, recv_page = [], [], [], []
    for k in range(1, inst):
        dst = lax.rem(me + k, inst)
        src = lax.rem(me + inst - k, inst)
        out_has = jnp.int32(0)
        out_row = jnp.int32(0)
        in_has = jnp.int32(0)
        in_move = jnp.int32(0)
        for m in range(move_count):
            goes = (sources[m] == me) & (moves[1, m] == dst)
            comes = (sources[m] == src) & (moves[1, m] == me)
            out_has = jnp.where(goes, 1, out_has)
            out_row = jnp.where(goes, moves[0, m] - me * row_count, out_row)
            in_has = jnp.where(comes, 1, in_has)
            in_move = jnp.where(comes, m, in_move)
        for j in range(per_rank):
            send_has.append(out_has)
            found = table[out_row, rank + tp * j] - rank * pages
            send_page.append(jnp.clip(found, 0, pages - 1))
            recv_has.append(in_has)
            recv_page.append(dests[in_move, rank + tp * j] - rank * pages)
    slots = (inst - 1) * per_rank
    plan = []
    for p in range(pages):
        source = jnp.int32(0)
        lands = jnp.int32(0)
        freed = jnp.int32(0)
        for i in range(slots):
            match = (recv_has[i] == 1) & (recv_page[i] == p)
            source = jnp.where(match, i, source)
            lands = jnp.where(match, 1, lands)
            freed = jnp.where((send_has[i] == 1) & (send_page[i] == p), 1, freed)
        plan.append((source, lands, freed))

    loads[7].wait()
    for copy in gathers:
        copy.wait_recv()

    def token_columns(c):
        at = c % cw
        if not isinstance(at, int):
            at = pl.multiple_of(at, hd)
        return full[c // cw, :, pl.ds(at, hd)]

    base = QUERY_HEADS * hd
    for which in range(2):
        for g in range(KEY_VALUE_HEADS):
            fresh = token_columns(base + which * width + g * hd)
            placed = jnp.dot(hit_t, fresh, preferred_element_type=jnp.float32)
            old = cache[:, which, :, g * hd : (g + 1) * hd].reshape(spots, hd)
            new = jnp.where(written, placed, old.astype(jnp.float32)).astype(jnp.bfloat16)
            cache[:, which, :, g * hd : (g + 1) * hd] = new.reshape(pages, extent, hd)

    page_copies = []
    for k in range(1, inst):
        for j in range(per_rank):
            outgoing[k - 1, j] = cache[send_page[(k - 1) * per_rank + j]]
        page_copies.append(
            pltpu.make_async_remote_copy(
                src_ref=outgoing.at[k - 1],
                dst_ref=arrived.at[k - 1],
                send_sem=page_send.at[k - 1],
                recv_sem=page_recv.at[k - 1],
                device_id={"inst": lax.rem(me + k, inst)},
                device_id_type=MESH,
            )
        )
    for copy in page_copies:
        copy.start()

    scale = 1.0 / math.sqrt(hd)
    lane = lax.broadcasted_iota(jnp.int32, (rows, 128), 1)

    def attend(g):
        queries = jnp.concatenate(
            [token_columns((g * group + j) * hd) for j in range(group)], axis=0
        )
        at = g * hd if isinstance(g, int) else pl.multiple_of(g * hd, hd)
        keys = cache[:, 0, :, pl.ds(at, hd)].reshape(spots, hd)
        values = cache[:, 1, :, pl.ds(at, hd)].reshape(spots, hd)
        scores = (
            lax.dot_general(
                queries, keys, (((1,), (1,)), ((), ())), preferred_element_type=jnp.float32
            )
            * scale
        )
        scores = jnp.where(visible_all, scores, NEG_LARGE)
        top = jnp.max(scores, axis=1, keepdims=True)
        exponent = jnp.where(visible_all, jnp.exp(scores - top), 0.0)
        total = jnp.sum(exponent, axis=1, keepdims=True)
        summed = jnp.dot(
            exponent.astype(jnp.bfloat16), values, preferred_element_type=jnp.float32
        ).astype(jnp.bfloat16)
        return top, total, summed

    def place(stats, at, j, top, total):
        take = slice(j * rows, (j + 1) * rows)
        stats = jnp.where(lane == at, top[take], stats)
        return jnp.where(lane == 64 + at, total[take], stats)

    sums = [
        (
            exchange(1, k, part.at[peers[k]], land.at[k - 1]),
            exchange(2, k, stat.at[peers[k]], land_stat.at[k - 1]),
        )
        for k in range(1, tp)
    ]
    for pair in sums:
        started += pair
    nothing = jnp.zeros((rows, 128), jnp.float32)
    if heads_per % group == 0:
        for k in list(reversed(range(1, tp))) + [0]:
            t = peers[k]
            stats = nothing
            for i in range(heads_per // group):
                top, total, summed = attend(t * (heads_per // group) + i)
                for j in range(group):
                    at = i * group + j
                    part[t, :, at * hd : (at + 1) * hd] = summed[j * rows : (j + 1) * rows]
                    stats = place(stats, at, j, top, total)
            stat[t] = stats
            if k:
                sums[k - 1][1].start()
                sums[k - 1][0].start()
    else:
        every = [nothing for _ in range(tp)]
        for g in range(KEY_VALUE_HEADS):
            top, total, summed = attend(g)
            for j in range(group):
                h = g * group + j
                t, at = h // heads_per, h % heads_per
                part[t, :, at * hd : (at + 1) * hd] = summed[j * rows : (j + 1) * rows]
                every[t] = place(every[t], at, j, top, total)
        for t in range(tp):
            stat[t] = every[t]
        for pair in sums:
            pair[1].start()
            pair[0].start()
    for pair in sums:
        pair[1].wait_recv()
        pair[0].wait_recv()

    all_stats = [stat[rank]] + [land_stat[k] for k in range(tp - 1)]
    highest = functools.reduce(jnp.maximum, all_stats)
    scales = [jnp.exp(s - highest) for s in all_stats]
    whole = functools.reduce(
        jnp.add, [pltpu.roll(s, 64, 1) * f for s, f in zip(all_stats, scales)]
    )
    whole = jnp.where(whole > 0.0, whole, 1.0)
    factors = [f / whole for f in scales]
    for at in range(heads_per):
        span = slice(at * hd, (at + 1) * hd)
        merged = part[rank, :, span].astype(jnp.float32) * factors[0][:, at : at + 1]
        for k in range(tp - 1):
            merged += land[k, :, span].astype(jnp.float32) * factors[k + 1][:, at : at + 1]
        mixed[rank, :, span] = merged.astype(jnp.bfloat16)

    shares = [exchange(3, k, mixed.at[rank], mixed.at[rank]) for k in range(1, tp)]
    for copy in reversed(shares):
        copy.start()
    started += shares

    columns = wbuf.shape[2]
    tile = min(256, columns)

    def project(k):
        t = froms[k]
        pltpu.make_async_copy(
            w_hbm.at[pl.ds(0, chunk), :], wbuf.at[t], w_sem.at[t]
        ).wait()

        def step(n, carry):
            span = pl.ds(pl.multiple_of(n * tile, tile), tile)
            product = jnp.dot(
                mixed[t], wbuf[t, :, span], preferred_element_type=jnp.float32
            )
            if k == 0:
                acc[:, span] = product
            else:
                acc[:, span] += product
            return carry

        lax.fori_loop(0, columns // tile, step, 0)

    def settle():
        for copy in page_copies:
            copy.wait_recv()
        for p in range(pages):
            source, lands, freed = plan[p]
            kept = jnp.where(freed == 1, jnp.zeros((), jnp.bfloat16), cache[p])
            if slots:
                kept = jnp.where(
                    lands == 1, arrived[source // per_rank, source % per_rank], kept
                )
            cache[p] = kept

    project(0)
    if tp == 1:
        settle()
    for k in range(1, tp):
        shares[k - 1].wait_recv()
        project(k)
        if k == 1:
            settle()
    o1_ref[...] = acc[0:row_count].astype(jnp.bfloat16)
    o2_ref[...] = acc[row_count : 2 * row_count].astype(jnp.bfloat16)
    for copy in started + page_copies:
        copy.wait_send()


def deliver(*refs):
    count = (len(refs) - 1) // 2
    sems = refs[-1]
    copies = [
        pltpu.make_async_copy(refs[i], refs[count + i], sems.at[i]) for i in range(count)
    ]
    for copy in copies:
        copy.start()
    for copy in copies:
        copy.wait()


def local(qkv_first, qkv_second, w_out, kv_cache, lengths, page_table, moves, dest_pages):
    tp = lax.axis_size("tp")
    inst = lax.axis_size("inst")
    row_count, max_pages = page_table.shape
    rows = -(-2 * row_count // 16) * 16
    cw = qkv_first.shape[1]
    columns = w_out.shape[1]
    share = QUERY_HEADS * HEAD_SIZE // tp
    per_rank = max_pages // tp
    sizes = (tp, inst, row_count, max_pages, moves.shape[0])
    vmem = pl.BlockSpec(memory_space=pltpu.VMEM)
    anywhere = pl.BlockSpec(memory_space=pl.ANY)
    page = kv_cache.shape[1:]
    bf16, f32, i32 = jnp.bfloat16, jnp.float32, jnp.int32
    others = max(tp - 1, 1)
    far = max(inst - 1, 1)
    dma = pltpu.SemaphoreType.DMA
    out_shapes = [(row_count, columns), (row_count, columns), kv_cache.shape]
    held = pl.pallas_call(
        functools.partial(kernel, sizes),
        out_shape=tuple(pltpu.VMEM(shape, bf16) for shape in out_shapes),
        in_specs=[anywhere] * 8,
        out_specs=(vmem, vmem, vmem),
        scratch_shapes=[
            pltpu.VMEM(qkv_first.shape, bf16),
            pltpu.VMEM(qkv_second.shape, bf16),
            pltpu.VMEM(page_table.shape, i32),
            pltpu.SMEM(lengths.shape, i32),
            pltpu.SMEM(moves.shape[::-1], i32),
            pltpu.SMEM(page_table.shape, i32),
            pltpu.SMEM(dest_pages.shape, i32),
            pltpu.VMEM((rows, cw), bf16),
            pltpu.VMEM((tp, rows, cw), bf16),
            pltpu.VMEM((tp, rows, share), bf16),
            pltpu.VMEM((tp, rows, 128), f32),
            pltpu.VMEM((others, rows, share), bf16),
            pltpu.VMEM((others, rows, 128), f32),
            pltpu.VMEM((tp, rows, share), bf16),
            pltpu.VMEM((rows, columns), f32),
            pltpu.VMEM((tp, share, columns), bf16),
            pltpu.VMEM((far, per_rank) + page, bf16),
            pltpu.VMEM((far, per_rank) + page, bf16),
            dma((8,)),
            dma((tp,)),
            dma((4, tp)),
            dma((4, tp)),
            dma((far,)),
            dma((far,)),
        ],
        compiler_params=pltpu.CompilerParams(
            collective_id=0, has_side_effects=True, vmem_limit_bytes=52 << 20
        ),
    )(
        *[
            pltpu.with_memory_space_constraint(a, pltpu.HBM)
            for a in (
                qkv_first,
                qkv_second,
                lengths,
                moves.T,
                page_table,
                dest_pages,
                kv_cache,
                w_out,
            )
        ]
    )
    return pl.pallas_call(
        deliver,
        out_shape=tuple(jax.ShapeDtypeStruct(shape, bf16) for shape in out_shapes),
        in_specs=[vmem] * 3,
        out_specs=(anywhere,) * 3,
        scratch_shapes=[dma((3,))],
        compiler_params=pltpu.CompilerParams(vmem_limit_bytes=1 << 20),
    )(*[pltpu.with_memory_space_constraint(h, pltpu.VMEM) for h in held])


def solution(mesh):
    placed = (
        P(("groups", "inst"), "tp"),
        P(("groups", "inst"), "tp"),
        P(None, "tp"),
        P(("groups", "inst", "tp"), None, None, None),
        P("groups"),
        P(("groups", "inst"), None),
        P("groups", None),
        P("groups", None),
    )
    return jax.shard_map(
        local,
        mesh=mesh,
        in_specs=placed,
        out_specs=(
            P(("groups", "inst"), "tp"),
            P(("groups", "inst"), "tp"),
            P(("groups", "inst", "tp"), None, None, None),
        ),
        check_vma=False,
    )
```

```python
import functools
import math

import jax
import jax.numpy as jnp
from jax import lax
from jax.experimental import pallas as pl
from jax.experimental.pallas import tpu as pltpu
from jax.sharding import PartitionSpec as P

QUERY_HEADS = 64
KEY_VALUE_HEADS = 8
HEAD_SIZE = 128
NEG_LARGE = -1e30
FAR = 1 << 30
MESH = pl.DeviceIdType.MESH


def partner(rank, k, count):
    if count & (count - 1):
        return lax.rem(rank + k, count), lax.rem(rank + count - k, count)
    other = jnp.int32(0)
    bit = 1
    while bit < count:
        mine = (rank // bit) % 2
        other = other + bit * ((1 - mine) if (k // bit) % 2 else mine)
        bit *= 2
    return other, other


def kernel(
    sizes,
    first_hbm,
    second_hbm,
    lengths_hbm,
    moves_hbm,
    table_hbm,
    dests_hbm,
    cache_hbm,
    w_hbm,
    o1_ref,
    o2_ref,
    cache,
    first,
    second,
    table_v,
    lengths,
    moves,
    table,
    dests,
    x_ref,
    full,
    part,
    stat,
    land,
    land_stat,
    mixed,
    acc,
    wbuf,
    outgoing,
    arrived,
    small_sem,
    w_sem,
    send_sem,
    recv_sem,
    page_send,
    page_recv,
):
    tp, inst, row_count, max_pages, move_count = sizes
    rank = lax.axis_index("tp")
    me = lax.axis_index("inst")
    rows, cw = x_ref.shape
    pages, _, extent, width = cache.shape
    spots = pages * extent
    heads_per = QUERY_HEADS // tp
    group = QUERY_HEADS // KEY_VALUE_HEADS
    hd = HEAD_SIZE
    per_rank = max_pages // tp
    chunk = wbuf.shape[1]
    peers = [partner(rank, k, tp)[0] for k in range(tp)]
    froms = [partner(rank, k, tp)[1] for k in range(tp)]

    loads = [
        pltpu.make_async_copy(src, dst, small_sem.at[i])
        for i, (src, dst) in enumerate(
            [
                (first_hbm, first),
                (second_hbm, second),
                (table_hbm, table_v),
                (lengths_hbm, lengths),
                (moves_hbm, moves),
                (table_hbm, table),
                (dests_hbm, dests),
                (cache_hbm, cache),
            ]
        )
    ]
    for load in loads:
        load.start()
    barrier = pltpu.get_barrier_semaphore()
    for k in range(1, tp):
        pl.semaphore_signal(
            barrier, inc=1, device_id={"tp": lax.rem(rank + k, tp)}, device_id_type=MESH
        )
    for k in range(1, inst):
        pl.semaphore_signal(
            barrier, inc=1, device_id={"inst": lax.rem(me + k, inst)}, device_id_type=MESH
        )
    for t in range(tp):
        pltpu.make_async_copy(
            w_hbm.at[pl.ds(t * chunk, chunk), :], wbuf.at[t], w_sem.at[t]
        ).start()
    loads[0].wait()
    loads[1].wait()
    pieces = [first[...].astype(jnp.float32), second[...].astype(jnp.float32)]
    if rows > 2 * row_count:
        pieces.append(jnp.zeros((rows - 2 * row_count, cw), jnp.float32))
    tokens = jnp.concatenate(pieces, axis=0).astype(jnp.bfloat16)
    x_ref[...] = tokens
    full[rank] = tokens
    pl.semaphore_wait(barrier, tp - 1 + inst - 1)

    def exchange(phase, k, src, dst):
        return pltpu.make_async_remote_copy(
            src_ref=src,
            dst_ref=dst,
            send_sem=send_sem.at[phase, k],
            recv_sem=recv_sem.at[phase, k],
            device_id={"tp": peers[k]},
            device_id_type=MESH,
        )

    relayed = tp >= 4 and tp & (tp - 1) == 0
    started = []

    def spread_out(phase, src, held):
        copies = {}
        order = list(range(2, tp)) + [1]
        for k in order:
            if relayed and k > 1 and k % 2:
                copies[k] = pltpu.make_async_remote_copy(
                    src_ref=held.at[froms[k - 1]],
                    dst_ref=held.at[froms[k - 1]],
                    send_sem=send_sem.at[phase, k],
                    recv_sem=recv_sem.at[phase, k],
                    device_id={"tp": peers[1]},
                    device_id_type=MESH,
                )
            else:
                copies[k] = exchange(phase, k, src, held.at[rank])
                copies[k].start()
            started.append(copies[k])
        return copies

    def arrive(copies, k):
        copies[k].wait_recv()
        if relayed and k > 1 and k % 2 == 0:
            copies[k + 1].start()

    gathers = spread_out(0, x_ref, full)
    for load in loads[2:7]:
        load.wait()

    column = lax.broadcasted_iota(jnp.int32, (row_count, spots), 1)
    page_id = column // extent + rank * pages
    offset = lax.rem(column, extent)
    pos = jnp.full((row_count, spots), FAR, jnp.int32)
    for n in range(max_pages):
        pos = jnp.where(table_v[:, n : n + 1] == page_id, n * extent + offset, pos)
    spread = [pos, pos]
    if rows > 2 * row_count:
        spread.append(jnp.full((rows - 2 * row_count, spots), FAR, jnp.int32))
    pos = jnp.concatenate(spread, axis=0)
    row_id = lax.broadcasted_iota(jnp.int32, (rows, spots), 0)
    target = jnp.full((rows, spots), -5, jnp.int32)
    for r in range(row_count):
        length = lengths[me * row_count + r]
        target = jnp.where(row_id == r, length, target)
        target = jnp.where(row_id == row_count + r, length + 1, target)
    visible = pos <= target
    hit = jnp.where(pos == target, 1.0, 0.0)
    hit_t = hit.T.astype(jnp.bfloat16)
    written = jnp.dot(
        hit_t, jnp.ones((rows, hd), jnp.bfloat16), preferred_element_type=jnp.float32
    ) > 0.5
    visible_all = jnp.concatenate([visible.astype(jnp.int32)] * group, axis=0) > 0

    sources = [moves[0, m] // row_count for m in range(move_count)]
    send_has, send_page, recv_has, recv_page = [], [], [], []
    for k in range(1, inst):
        dst = lax.rem(me + k, inst)
        src = lax.rem(me + inst - k, inst)
        out_has = jnp.int32(0)
        out_row = jnp.int32(0)
        in_has = jnp.int32(0)
        in_move = jnp.int32(0)
        for m in range(move_count):
            goes = (sources[m] == me) & (moves[1, m] == dst)
            comes = (sources[m] == src) & (moves[1, m] == me)
            out_has = jnp.where(goes, 1, out_has)
            out_row = jnp.where(goes, moves[0, m] - me * row_count, out_row)
            in_has = jnp.where(comes, 1, in_has)
            in_move = jnp.where(comes, m, in_move)
        for j in range(per_rank):
            send_has.append(out_has)
            found = table[out_row, rank + tp * j] - rank * pages
            send_page.append(jnp.clip(found, 0, pages - 1))
            recv_has.append(in_has)
            recv_page.append(dests[in_move, rank + tp * j] - rank * pages)
    slots = (inst - 1) * per_rank
    plan = []
    for p in range(pages):
        source = jnp.int32(0)
        lands = jnp.int32(0)
        freed = jnp.int32(0)
        for i in range(slots):
            match = (recv_has[i] == 1) & (recv_page[i] == p)
            source = jnp.where(match, i, source)
            lands = jnp.where(match, 1, lands)
            freed = jnp.where((send_has[i] == 1) & (send_page[i] == p), 1, freed)
        plan.append((source, lands, freed))

    loads[7].wait()
    for k in [*range(2, tp, 2), 1, *range(3, tp, 2)] if relayed else range(1, tp):
        arrive(gathers, k)

    def token_columns(c):
        at = c % cw
        if not isinstance(at, int):
            at = pl.multiple_of(at, hd)
        return full[c // cw, :, pl.ds(at, hd)]

    base = QUERY_HEADS * hd
    for which in range(2):
        for g in range(KEY_VALUE_HEADS):
            fresh = token_columns(base + which * width + g * hd)
            placed = jnp.dot(hit_t, fresh, preferred_element_type=jnp.float32)
            old = cache[:, which, :, g * hd : (g + 1) * hd].reshape(spots, hd)
            new = jnp.where(written, placed, old.astype(jnp.float32)).astype(jnp.bfloat16)
            cache[:, which, :, g * hd : (g + 1) * hd] = new.reshape(pages, extent, hd)

    page_copies = []
    for k in range(1, inst):
        for j in range(per_rank):
            outgoing[k - 1, j] = cache[send_page[(k - 1) * per_rank + j]]
        page_copies.append(
            pltpu.make_async_remote_copy(
                src_ref=outgoing.at[k - 1],
                dst_ref=arrived.at[k - 1],
                send_sem=page_send.at[k - 1],
                recv_sem=page_recv.at[k - 1],
                device_id={"inst": lax.rem(me + k, inst)},
                device_id_type=MESH,
            )
        )
    for copy in page_copies:
        copy.start()

    scale = 1.0 / math.sqrt(hd)
    lane = lax.broadcasted_iota(jnp.int32, (rows, 128), 1)

    def attend(g):
        queries = jnp.concatenate(
            [token_columns((g * group + j) * hd) for j in range(group)], axis=0
        )
        at = g * hd if isinstance(g, int) else pl.multiple_of(g * hd, hd)
        keys = cache[:, 0, :, pl.ds(at, hd)].reshape(spots, hd)
        values = cache[:, 1, :, pl.ds(at, hd)].reshape(spots, hd)
        scores = (
            lax.dot_general(
                queries, keys, (((1,), (1,)), ((), ())), preferred_element_type=jnp.float32
            )
            * scale
        )
        scores = jnp.where(visible_all, scores, NEG_LARGE)
        top = jnp.max(scores, axis=1, keepdims=True)
        exponent = jnp.where(visible_all, jnp.exp(scores - top), 0.0)
        total = jnp.sum(exponent, axis=1, keepdims=True)
        summed = jnp.dot(
            exponent.astype(jnp.bfloat16), values, preferred_element_type=jnp.float32
        ).astype(jnp.bfloat16)
        return top, total, summed

    def place(stats, at, j, top, total):
        take = slice(j * rows, (j + 1) * rows)
        stats = jnp.where(lane == at, top[take], stats)
        return jnp.where(lane == 64 + at, total[take], stats)

    sums = [
        (
            exchange(1, k, part.at[peers[k]], land.at[k - 1]),
            exchange(2, k, stat.at[peers[k]], land_stat.at[k - 1]),
        )
        for k in range(1, tp)
    ]
    for pair in sums:
        started += pair
    nothing = jnp.zeros((rows, 128), jnp.float32)
    if heads_per % group == 0:
        for k in list(reversed(range(1, tp))) + [0]:
            t = peers[k]
            stats = nothing
            for i in range(heads_per // group):
                top, total, summed = attend(t * (heads_per // group) + i)
                for j in range(group):
                    at = i * group + j
                    part[t, :, at * hd : (at + 1) * hd] = summed[j * rows : (j + 1) * rows]
                    stats = place(stats, at, j, top, total)
            stat[t] = stats
            if k:
                sums[k - 1][1].start()
                sums[k - 1][0].start()
    else:
        every = [nothing for _ in range(tp)]
        for g in range(KEY_VALUE_HEADS):
            top, total, summed = attend(g)
            for j in range(group):
                h = g * group + j
                t, at = h // heads_per, h % heads_per
                part[t, :, at * hd : (at + 1) * hd] = summed[j * rows : (j + 1) * rows]
                every[t] = place(every[t], at, j, top, total)
        for t in range(tp):
            stat[t] = every[t]
        for pair in sums:
            pair[1].start()
            pair[0].start()
    for pair in sums:
        pair[1].wait_recv()
        pair[0].wait_recv()

    all_stats = [stat[rank]] + [land_stat[k] for k in range(tp - 1)]
    highest = functools.reduce(jnp.maximum, all_stats)
    scales = [jnp.exp(s - highest) for s in all_stats]
    whole = functools.reduce(
        jnp.add, [pltpu.roll(s, 64, 1) * f for s, f in zip(all_stats, scales)]
    )
    whole = jnp.where(whole > 0.0, whole, 1.0)
    factors = [f / whole for f in scales]
    for at in range(heads_per):
        span = slice(at * hd, (at + 1) * hd)
        merged = part[rank, :, span].astype(jnp.float32) * factors[0][:, at : at + 1]
        for k in range(tp - 1):
            merged += land[k, :, span].astype(jnp.float32) * factors[k + 1][:, at : at + 1]
        mixed[rank, :, span] = merged.astype(jnp.bfloat16)

    shares = spread_out(3, mixed.at[rank], mixed)

    columns = wbuf.shape[2]
    tile = columns

    def project(k):
        t = froms[k]
        pltpu.make_async_copy(
            w_hbm.at[pl.ds(0, chunk), :], wbuf.at[t], w_sem.at[t]
        ).wait()

        def step(n, carry):
            span = pl.ds(pl.multiple_of(n * tile, tile), tile)
            product = jnp.dot(
                mixed[t], wbuf[t, :, span], preferred_element_type=jnp.float32
            )
            if k == 0:
                acc[:, span] = product
            else:
                acc[:, span] += product
            return carry

        lax.fori_loop(0, columns // tile, step, 0)

    def settle():
        for copy in page_copies:
            copy.wait_recv()
        for p in range(pages):
            source, lands, freed = plan[p]
            kept = jnp.where(freed == 1, jnp.zeros((), jnp.bfloat16), cache[p])
            if slots:
                kept = jnp.where(
                    lands == 1, arrived[source // per_rank, source % per_rank], kept
                )
            cache[p] = kept

    project(0)
    for k in range(1, tp):
        arrive(shares, k)
        project(k)
    settle()
    o1_ref[...] = acc[0:row_count].astype(jnp.bfloat16)
    o2_ref[...] = acc[row_count : 2 * row_count].astype(jnp.bfloat16)
    for copy in started + page_copies:
        copy.wait_send()


def deliver(*refs):
    count = (len(refs) - 1) // 2
    sems = refs[-1]
    copies = [
        pltpu.make_async_copy(refs[i], refs[count + i], sems.at[i]) for i in range(count)
    ]
    for copy in copies:
        copy.start()
    for copy in copies:
        copy.wait()


def local(qkv_first, qkv_second, w_out, kv_cache, lengths, page_table, moves, dest_pages):
    tp = lax.axis_size("tp")
    inst = lax.axis_size("inst")
    row_count, max_pages = page_table.shape
    rows = -(-2 * row_count // 16) * 16
    cw = qkv_first.shape[1]
    columns = w_out.shape[1]
    share = QUERY_HEADS * HEAD_SIZE // tp
    per_rank = max_pages // tp
    sizes = (tp, inst, row_count, max_pages, moves.shape[0])
    vmem = pl.BlockSpec(memory_space=pltpu.VMEM)
    anywhere = pl.BlockSpec(memory_space=pl.ANY)
    page = kv_cache.shape[1:]
    bf16, f32, i32 = jnp.bfloat16, jnp.float32, jnp.int32
    others = max(tp - 1, 1)
    far = max(inst - 1, 1)
    dma = pltpu.SemaphoreType.DMA
    out_shapes = [(row_count, columns), (row_count, columns), kv_cache.shape]
    held = pl.pallas_call(
        functools.partial(kernel, sizes),
        out_shape=tuple(pltpu.VMEM(shape, bf16) for shape in out_shapes),
        in_specs=[anywhere] * 8,
        out_specs=(vmem, vmem, vmem),
        scratch_shapes=[
            pltpu.VMEM(qkv_first.shape, bf16),
            pltpu.VMEM(qkv_second.shape, bf16),
            pltpu.VMEM(page_table.shape, i32),
            pltpu.SMEM(lengths.shape, i32),
            pltpu.SMEM(moves.shape[::-1], i32),
            pltpu.SMEM(page_table.shape, i32),
            pltpu.SMEM(dest_pages.shape, i32),
            pltpu.VMEM((rows, cw), bf16),
            pltpu.VMEM((tp, rows, cw), bf16),
            pltpu.VMEM((tp, rows, share), bf16),
            pltpu.VMEM((tp, rows, 128), f32),
            pltpu.VMEM((others, rows, share), bf16),
            pltpu.VMEM((others, rows, 128), f32),
            pltpu.VMEM((tp, rows, share), bf16),
            pltpu.VMEM((rows, columns), f32),
            pltpu.VMEM((tp, share, columns), bf16),
            pltpu.VMEM((far, per_rank) + page, bf16),
            pltpu.VMEM((far, per_rank) + page, bf16),
            dma((8,)),
            dma((tp,)),
            dma((4, tp)),
            dma((4, tp)),
            dma((far,)),
            dma((far,)),
        ],
        compiler_params=pltpu.CompilerParams(
            collective_id=0, has_side_effects=True, vmem_limit_bytes=52 << 20
        ),
    )(
        *[
            pltpu.with_memory_space_constraint(a, pltpu.HBM)
            for a in (
                qkv_first,
                qkv_second,
                lengths,
                moves.T,
                page_table,
                dest_pages,
                kv_cache,
                w_out,
            )
        ]
    )
    return pl.pallas_call(
        deliver,
        out_shape=tuple(jax.ShapeDtypeStruct(shape, bf16) for shape in out_shapes),
        in_specs=[vmem] * 3,
        out_specs=(anywhere,) * 3,
        scratch_shapes=[dma((3,))],
        compiler_params=pltpu.CompilerParams(vmem_limit_bytes=1 << 20),
    )(*[pltpu.with_memory_space_constraint(h, pltpu.VMEM) for h in held])


def solution(mesh):
    placed = (
        P(("groups", "inst"), "tp"),
        P(("groups", "inst"), "tp"),
        P(None, "tp"),
        P(("groups", "inst", "tp"), None, None, None),
        P("groups"),
        P(("groups", "inst"), None),
        P("groups", None),
        P("groups", None),
    )
    return jax.shard_map(
        local,
        mesh=mesh,
        in_specs=placed,
        out_specs=(
            P(("groups", "inst"), "tp"),
            P(("groups", "inst"), "tp"),
            P(("groups", "inst", "tp"), None, None, None),
        ),
        check_vma=False,
    )
```

```python
import functools
import math

import jax
import jax.numpy as jnp
from jax import lax
from jax.experimental import pallas as pl
from jax.experimental.pallas import tpu as pltpu
from jax.sharding import PartitionSpec as P

QUERY_HEADS = 64
KEY_VALUE_HEADS = 8
HEAD_SIZE = 128
NEG_LARGE = -1e30
FAR = 1 << 30
MESH = pl.DeviceIdType.MESH


def partner(rank, k, count):
    if count & (count - 1):
        return lax.rem(rank + k, count), lax.rem(rank + count - k, count)
    other = jnp.int32(0)
    bit = 1
    while bit < count:
        mine = (rank // bit) % 2
        other = other + bit * ((1 - mine) if (k // bit) % 2 else mine)
        bit *= 2
    return other, other


def kernel(
    sizes,
    first_hbm,
    second_hbm,
    lengths_hbm,
    moves_hbm,
    table_hbm,
    dests_hbm,
    cache_hbm,
    w_hbm,
    o1_ref,
    o2_ref,
    cache,
    first,
    second,
    table_v,
    lengths,
    moves,
    table,
    dests,
    x_ref,
    full,
    part,
    stat,
    land,
    land_stat,
    mixed,
    acc,
    wbuf,
    outgoing,
    arrived,
    small_sem,
    w_sem,
    send_sem,
    recv_sem,
    page_send,
    page_recv,
):
    tp, inst, row_count, max_pages, move_count = sizes
    rank = lax.axis_index("tp")
    me = lax.axis_index("inst")
    rows, cw = x_ref.shape
    pages, _, extent, width = cache.shape
    spots = pages * extent
    heads_per = QUERY_HEADS // tp
    group = QUERY_HEADS // KEY_VALUE_HEADS
    hd = HEAD_SIZE
    per_rank = max_pages // tp
    chunk = wbuf.shape[1]
    peers = [partner(rank, k, tp)[0] for k in range(tp)]
    froms = [partner(rank, k, tp)[1] for k in range(tp)]

    loads = [
        pltpu.make_async_copy(src, dst, small_sem.at[i])
        for i, (src, dst) in enumerate(
            [
                (first_hbm, first),
                (second_hbm, second),
                (table_hbm, table_v),
                (lengths_hbm, lengths),
                (moves_hbm, moves),
                (table_hbm, table),
                (dests_hbm, dests),
                (cache_hbm, cache),
            ]
        )
    ]
    for load in loads:
        load.start()
    barrier = pltpu.get_barrier_semaphore()
    for k in range(1, tp):
        pl.semaphore_signal(
            barrier, inc=1, device_id={"tp": lax.rem(rank + k, tp)}, device_id_type=MESH
        )
    for k in range(1, inst):
        pl.semaphore_signal(
            barrier, inc=1, device_id={"inst": lax.rem(me + k, inst)}, device_id_type=MESH
        )
    for t in range(tp):
        pltpu.make_async_copy(
            w_hbm.at[pl.ds(t * chunk, chunk), :], wbuf.at[t], w_sem.at[t]
        ).start()
    loads[0].wait()
    loads[1].wait()
    pieces = [first[...].astype(jnp.float32), second[...].astype(jnp.float32)]
    if rows > 2 * row_count:
        pieces.append(jnp.zeros((rows - 2 * row_count, cw), jnp.float32))
    tokens = jnp.concatenate(pieces, axis=0).astype(jnp.bfloat16)
    x_ref[...] = tokens
    full[rank] = tokens
    pl.semaphore_wait(barrier, tp - 1 + inst - 1)

    def exchange(phase, k, src, dst):
        return pltpu.make_async_remote_copy(
            src_ref=src,
            dst_ref=dst,
            send_sem=send_sem.at[phase, k],
            recv_sem=recv_sem.at[phase, k],
            device_id={"tp": peers[k]},
            device_id_type=MESH,
        )

    relayed = tp >= 4 and tp & (tp - 1) == 0
    started = []

    def spread_out(phase, src, held):
        copies = {}
        order = list(range(2, tp)) + [1]
        for k in order:
            if relayed and k > 1 and k % 2:
                copies[k] = pltpu.make_async_remote_copy(
                    src_ref=held.at[froms[k - 1]],
                    dst_ref=held.at[froms[k - 1]],
                    send_sem=send_sem.at[phase, k],
                    recv_sem=recv_sem.at[phase, k],
                    device_id={"tp": peers[1]},
                    device_id_type=MESH,
                )
            else:
                copies[k] = exchange(phase, k, src, held.at[rank])
                copies[k].start()
            started.append(copies[k])
        return copies

    def arrive(copies, k):
        copies[k].wait_recv()
        if relayed and k > 1 and k % 2 == 0:
            copies[k + 1].start()

    gathers = spread_out(0, x_ref, full)
    for load in loads[2:7]:
        load.wait()

    column = lax.broadcasted_iota(jnp.int32, (row_count, spots), 1)
    page_id = column // extent + rank * pages
    offset = lax.rem(column, extent)
    pos = jnp.full((row_count, spots), FAR, jnp.int32)
    for n in range(max_pages):
        pos = jnp.where(table_v[:, n : n + 1] == page_id, n * extent + offset, pos)
    spread = [pos, pos]
    if rows > 2 * row_count:
        spread.append(jnp.full((rows - 2 * row_count, spots), FAR, jnp.int32))
    pos = jnp.concatenate(spread, axis=0)
    row_id = lax.broadcasted_iota(jnp.int32, (rows, spots), 0)
    target = jnp.full((rows, spots), -5, jnp.int32)
    for r in range(row_count):
        length = lengths[me * row_count + r]
        target = jnp.where(row_id == r, length, target)
        target = jnp.where(row_id == row_count + r, length + 1, target)
    visible = pos <= target
    hit = jnp.where(pos == target, 1.0, 0.0)
    hit_t = hit.T.astype(jnp.bfloat16)
    written = jnp.dot(
        hit_t, jnp.ones((rows, hd), jnp.bfloat16), preferred_element_type=jnp.float32
    ) > 0.5
    visible_all = jnp.concatenate([visible.astype(jnp.int32)] * group, axis=0) > 0

    sources = [moves[0, m] // row_count for m in range(move_count)]
    send_has, send_page, recv_has, recv_page = [], [], [], []
    for k in range(1, inst):
        dst = lax.rem(me + k, inst)
        src = lax.rem(me + inst - k, inst)
        out_has = jnp.int32(0)
        out_row = jnp.int32(0)
        in_has = jnp.int32(0)
        in_move = jnp.int32(0)
        for m in range(move_count):
            goes = (sources[m] == me) & (moves[1, m] == dst)
            comes = (sources[m] == src) & (moves[1, m] == me)
            out_has = jnp.where(goes, 1, out_has)
            out_row = jnp.where(goes, moves[0, m] - me * row_count, out_row)
            in_has = jnp.where(comes, 1, in_has)
            in_move = jnp.where(comes, m, in_move)
        for j in range(per_rank):
            send_has.append(out_has)
            found = table[out_row, rank + tp * j] - rank * pages
            send_page.append(jnp.clip(found, 0, pages - 1))
            recv_has.append(in_has)
            recv_page.append(dests[in_move, rank + tp * j] - rank * pages)
    slots = (inst - 1) * per_rank
    plan = []
    for p in range(pages):
        source = jnp.int32(0)
        lands = jnp.int32(0)
        freed = jnp.int32(0)
        for i in range(slots):
            match = (recv_has[i] == 1) & (recv_page[i] == p)
            source = jnp.where(match, i, source)
            lands = jnp.where(match, 1, lands)
            freed = jnp.where((send_has[i] == 1) & (send_page[i] == p), 1, freed)
        plan.append((source, lands, freed))

    loads[7].wait()
    for k in [*range(2, tp, 2), 1, *range(3, tp, 2)] if relayed else range(1, tp):
        arrive(gathers, k)

    def token_columns(c):
        at = c % cw
        if not isinstance(at, int):
            at = pl.multiple_of(at, hd)
        return full[c // cw, :, pl.ds(at, hd)]

    base = QUERY_HEADS * hd
    for which in range(2):
        for g in range(KEY_VALUE_HEADS):
            fresh = token_columns(base + which * width + g * hd)
            placed = jnp.dot(hit_t, fresh, preferred_element_type=jnp.float32)
            old = cache[:, which, :, g * hd : (g + 1) * hd].reshape(spots, hd)
            new = jnp.where(written, placed, old.astype(jnp.float32)).astype(jnp.bfloat16)
            cache[:, which, :, g * hd : (g + 1) * hd] = new.reshape(pages, extent, hd)

    page_copies = []
    for k in range(1, inst):
        for j in range(per_rank):
            outgoing[k - 1, j] = cache[send_page[(k - 1) * per_rank + j]]
        page_copies.append(
            pltpu.make_async_remote_copy(
                src_ref=outgoing.at[k - 1],
                dst_ref=arrived.at[k - 1],
                send_sem=page_send.at[k - 1],
                recv_sem=page_recv.at[k - 1],
                device_id={"inst": lax.rem(me + k, inst)},
                device_id_type=MESH,
            )
        )
    for copy in page_copies:
        copy.start()

    scale = 1.0 / math.sqrt(hd)
    lane = lax.broadcasted_iota(jnp.int32, (rows, 128), 1)

    def attend(g):
        queries = jnp.concatenate(
            [token_columns((g * group + j) * hd) for j in range(group)], axis=0
        )
        at = g * hd if isinstance(g, int) else pl.multiple_of(g * hd, hd)
        keys = cache[:, 0, :, pl.ds(at, hd)].reshape(spots, hd)
        values = cache[:, 1, :, pl.ds(at, hd)].reshape(spots, hd)
        scores = (
            lax.dot_general(
                queries, keys, (((1,), (1,)), ((), ())), preferred_element_type=jnp.float32
            )
            * scale
        )
        scores = jnp.where(visible_all, scores, NEG_LARGE)
        top = jnp.max(scores, axis=1, keepdims=True)
        exponent = jnp.where(visible_all, jnp.exp(scores - top), 0.0)
        total = jnp.sum(exponent, axis=1, keepdims=True)
        summed = jnp.dot(
            exponent.astype(jnp.bfloat16), values, preferred_element_type=jnp.float32
        ).astype(jnp.bfloat16)
        return top, total, summed

    def place(stats, at, j, top, total):
        take = slice(j * rows, (j + 1) * rows)
        stats = jnp.where(lane == at, top[take], stats)
        return jnp.where(lane == 64 + at, total[take], stats)

    sums = [
        (
            exchange(1, k, part.at[peers[k]], land.at[k - 1]),
            exchange(2, k, stat.at[peers[k]], land_stat.at[k - 1]),
        )
        for k in range(1, tp)
    ]
    for pair in sums:
        started += pair
    nothing = jnp.zeros((rows, 128), jnp.float32)
    if heads_per % group == 0:
        for k in list(reversed(range(1, tp))) + [0]:
            t = peers[k]
            stats = nothing
            for i in range(heads_per // group):
                top, total, summed = attend(t * (heads_per // group) + i)
                for j in range(group):
                    at = i * group + j
                    part[t, :, at * hd : (at + 1) * hd] = summed[j * rows : (j + 1) * rows]
                    stats = place(stats, at, j, top, total)
            stat[t] = stats
            if k:
                sums[k - 1][1].start()
                sums[k - 1][0].start()
    else:
        every = [nothing for _ in range(tp)]
        for g in range(KEY_VALUE_HEADS):
            top, total, summed = attend(g)
            for j in range(group):
                h = g * group + j
                t, at = h // heads_per, h % heads_per
                part[t, :, at * hd : (at + 1) * hd] = summed[j * rows : (j + 1) * rows]
                every[t] = place(every[t], at, j, top, total)
        for t in range(tp):
            stat[t] = every[t]
        for pair in sums:
            pair[1].start()
            pair[0].start()
    for pair in sums:
        pair[1].wait_recv()
        pair[0].wait_recv()

    all_stats = [stat[rank]] + [land_stat[k] for k in range(tp - 1)]
    highest = functools.reduce(jnp.maximum, all_stats)
    scales = [jnp.exp(s - highest) for s in all_stats]
    whole = functools.reduce(
        jnp.add, [pltpu.roll(s, 64, 1) * f for s, f in zip(all_stats, scales)]
    )
    whole = jnp.where(whole > 0.0, whole, 1.0)
    factors = [f / whole for f in scales]
    for at in range(heads_per):
        span = slice(at * hd, (at + 1) * hd)
        merged = part[rank, :, span].astype(jnp.float32) * factors[0][:, at : at + 1]
        for k in range(tp - 1):
            merged += land[k, :, span].astype(jnp.float32) * factors[k + 1][:, at : at + 1]
        mixed[rank, :, span] = merged.astype(jnp.bfloat16)

    shares = spread_out(3, mixed.at[rank], mixed)

    columns = wbuf.shape[2]
    tile = columns

    def project(k):
        t = froms[k]
        pltpu.make_async_copy(
            w_hbm.at[pl.ds(0, chunk), :], wbuf.at[t], w_sem.at[t]
        ).wait()

        def step(n, carry):
            span = pl.ds(pl.multiple_of(n * tile, tile), tile)
            product = jnp.dot(
                mixed[t], wbuf[t, :, span], preferred_element_type=jnp.float32
            )
            if k == 0:
                acc[:, span] = product
            else:
                acc[:, span] += product
            return carry

        lax.fori_loop(0, columns // tile, step, 0)

    def settle():
        for copy in page_copies:
            copy.wait_recv()
        for p in range(pages):
            source, lands, freed = plan[p]
            kept = jnp.where(freed == 1, jnp.zeros((), jnp.bfloat16), cache[p])
            if slots:
                kept = jnp.where(
                    lands == 1, arrived[source // per_rank, source % per_rank], kept
                )
            cache[p] = kept

    project(0)
    for k in range(1, tp):
        if k == tp - 1:
            settle()
        arrive(shares, k)
        project(k)
    if tp == 1:
        settle()
    o1_ref[...] = acc[0:row_count].astype(jnp.bfloat16)
    o2_ref[...] = acc[row_count : 2 * row_count].astype(jnp.bfloat16)
    for copy in started + page_copies:
        copy.wait_send()


def deliver(*refs):
    count = (len(refs) - 1) // 2
    sems = refs[-1]
    copies = [
        pltpu.make_async_copy(refs[i], refs[count + i], sems.at[i]) for i in range(count)
    ]
    for copy in copies:
        copy.start()
    for copy in copies:
        copy.wait()


def local(qkv_first, qkv_second, w_out, kv_cache, lengths, page_table, moves, dest_pages):
    tp = lax.axis_size("tp")
    inst = lax.axis_size("inst")
    row_count, max_pages = page_table.shape
    rows = -(-2 * row_count // 16) * 16
    cw = qkv_first.shape[1]
    columns = w_out.shape[1]
    share = QUERY_HEADS * HEAD_SIZE // tp
    per_rank = max_pages // tp
    sizes = (tp, inst, row_count, max_pages, moves.shape[0])
    vmem = pl.BlockSpec(memory_space=pltpu.VMEM)
    anywhere = pl.BlockSpec(memory_space=pl.ANY)
    page = kv_cache.shape[1:]
    bf16, f32, i32 = jnp.bfloat16, jnp.float32, jnp.int32
    others = max(tp - 1, 1)
    far = max(inst - 1, 1)
    dma = pltpu.SemaphoreType.DMA
    out_shapes = [(row_count, columns), (row_count, columns), kv_cache.shape]
    held = pl.pallas_call(
        functools.partial(kernel, sizes),
        out_shape=tuple(pltpu.VMEM(shape, bf16) for shape in out_shapes),
        in_specs=[anywhere] * 8,
        out_specs=(vmem, vmem, vmem),
        scratch_shapes=[
            pltpu.VMEM(qkv_first.shape, bf16),
            pltpu.VMEM(qkv_second.shape, bf16),
            pltpu.VMEM(page_table.shape, i32),
            pltpu.SMEM(lengths.shape, i32),
            pltpu.SMEM(moves.shape[::-1], i32),
            pltpu.SMEM(page_table.shape, i32),
            pltpu.SMEM(dest_pages.shape, i32),
            pltpu.VMEM((rows, cw), bf16),
            pltpu.VMEM((tp, rows, cw), bf16),
            pltpu.VMEM((tp, rows, share), bf16),
            pltpu.VMEM((tp, rows, 128), f32),
            pltpu.VMEM((others, rows, share), bf16),
            pltpu.VMEM((others, rows, 128), f32),
            pltpu.VMEM((tp, rows, share), bf16),
            pltpu.VMEM((rows, columns), f32),
            pltpu.VMEM((tp, share, columns), bf16),
            pltpu.VMEM((far, per_rank) + page, bf16),
            pltpu.VMEM((far, per_rank) + page, bf16),
            dma((8,)),
            dma((tp,)),
            dma((4, tp)),
            dma((4, tp)),
            dma((far,)),
            dma((far,)),
        ],
        compiler_params=pltpu.CompilerParams(
            collective_id=0, has_side_effects=True, vmem_limit_bytes=52 << 20
        ),
    )(
        *[
            pltpu.with_memory_space_constraint(a, pltpu.HBM)
            for a in (
                qkv_first,
                qkv_second,
                lengths,
                moves.T,
                page_table,
                dest_pages,
                kv_cache,
                w_out,
            )
        ]
    )
    return pl.pallas_call(
        deliver,
        out_shape=tuple(jax.ShapeDtypeStruct(shape, bf16) for shape in out_shapes),
        in_specs=[vmem] * 3,
        out_specs=(anywhere,) * 3,
        scratch_shapes=[dma((3,))],
        compiler_params=pltpu.CompilerParams(vmem_limit_bytes=1 << 20),
    )(*[pltpu.with_memory_space_constraint(h, pltpu.VMEM) for h in held])


def solution(mesh):
    placed = (
        P(("groups", "inst"), "tp"),
        P(("groups", "inst"), "tp"),
        P(None, "tp"),
        P(("groups", "inst", "tp"), None, None, None),
        P("groups"),
        P(("groups", "inst"), None),
        P("groups", None),
        P("groups", None),
    )
    return jax.shard_map(
        local,
        mesh=mesh,
        in_specs=placed,
        out_specs=(
            P(("groups", "inst"), "tp"),
            P(("groups", "inst"), "tp"),
            P(("groups", "inst", "tp"), None, None, None),
        ),
        check_vma=False,
    )
```
